32 devices in a mesh: grp: 2 (over x), seq: 16 (over z, y, core).
Axes of the slice: x: 2, y: 2, z: 4, core: 2. Of those that a mesh axis runs over, the one named last changes fastest.
Arguments:
- tokens: bfloat16 [16384, 1024], P(('grp', 'seq')), parts along dimension 0, may hold values from -6 to 6
- value_weight: bfloat16 [1024, 1024], replicated, may hold values from -0.1875 to 0.1875
- gate_weight: bfloat16 [1024, 1024], replicated, may hold values from -0.1875 to 0.1875
- out_weight: bfloat16 [1024, 1024], replicated, may hold values from -0.1875 to 0.1875
- kernel_weight: bfloat16 [1024, 16], replicated, may hold values from -0.1875 to 0.1875
- kernel_bias: float32 [16], replicated, may hold values from -4 to 4
Outputs:
- mixed: bfloat16 [16384, 1024], P(('grp', 'seq')), parts along dimension 0
The draws below stay inside these ranges and needn't reach their ends.
There are 2 independent parts, one for each index of `grp`. The reference program is written for one: setup_inputs(seed, part) draws one part's arguments, and reference() takes and returns one part's arrays. A program takes and returns all parts, laid end to end along the dimension named above; an argument that names none is the same for every part. Nothing has to cross between parts.
All inputs are finite; a program needn't handle non-finite values.
Results may differ from the reference program's by a relative error of at most 0.0071.
Values may be sent and summed in bfloat16 or wider, within the bound.
A program may use at most 128 MiB of HBM per device.

```python
import jax
import jax.numpy as jnp

D = 1024
HEADS = 16
HS = 64
TOKENS = 8192


def block_levels(rng, extent, split, low, top_value):
    def one(position, blocks):
        steps = jax.random.uniform(jax.random.fold_in(jax.random.fold_in(rng, 6), position), (blocks,), jnp.float32, low / len(split), top_value / len(split))
        return jnp.repeat(jnp.exp(steps), extent[position] // blocks).reshape((-1,) + (1,) * (len(extent) - position - 1))

    factor_of = one(*split[0])
    for cut in split[1:]:
        factor_of = factor_of * one(*cut)
    return factor_of


def scatter_about(rng, dims, width, reach, split=(), dtype=jnp.bfloat16):
    level = block_levels(rng, dims, split, -0.22, 0.18) if split else 1.0
    array = jax.random.normal(rng, dims, jnp.float32) * width * level
    return jnp.minimum(jnp.maximum(array, -reach), reach).astype(dtype)


def setup_inputs(seed: int = 0, part: int = 0) -> dict:
    arg_keys = jax.random.split(jax.random.key(seed), 7)
    own_keys = jax.random.split(jax.random.fold_in(arg_keys[6], part), 7)
    tokens = scatter_about(own_keys[0], (TOKENS, D), 1.0, 6.0, ((0, 16),))
    value_weight = scatter_about(arg_keys[1], (D, D), D ** -0.5, 0.1875)
    gate_weight = scatter_about(arg_keys[2], (D, D), D ** -0.5, 0.1875)
    out_weight = scatter_about(arg_keys[3], (D, D), D ** -0.5, 0.1875)
    kernel_weight = scatter_about(arg_keys[4], (D, HEADS), D ** -0.5, 0.1875)
    kernel_bias = scatter_about(arg_keys[5], (HEADS,), 1.0, 4.0, (), jnp.float32)
    return dict(tokens=tokens, value_weight=value_weight, gate_weight=gate_weight, out_weight=out_weight, kernel_weight=kernel_weight, kernel_bias=kernel_bias)


def reference(tokens, value_weight, gate_weight, out_weight, kernel_weight, kernel_bias):
    values = jnp.dot(tokens, value_weight, preferred_element_type=jnp.float32).astype(jnp.bfloat16)
    gate = jnp.dot(tokens, gate_weight, preferred_element_type=jnp.float32)
    logits = jnp.dot(tokens, kernel_weight, preferred_element_type=jnp.float32) + kernel_bias
    kernel = (jnp.tanh(logits) * (TOKENS ** -0.5)).astype(jnp.bfloat16)
    kernel_freq = jnp.fft.rfft(kernel.astype(jnp.float32), axis=0)
    value_freq = jnp.fft.rfft(values.astype(jnp.float32), axis=0)
    product = value_freq.reshape(-1, HEADS, HS) * kernel_freq[:, :, None]
    conv = jnp.fft.irfft(product, n=TOKENS, axis=0).reshape(TOKENS, D).astype(jnp.bfloat16)
    gated = (conv.astype(jnp.float32) * jax.nn.silu(gate)).astype(jnp.bfloat16)
    return jnp.dot(gated, out_weight, preferred_element_type=jnp.float32).astype(jnp.bfloat16)
```

```python
import functools

import jax
import jax.numpy as jnp
from jax import lax
from jax.experimental import pallas as pl
from jax.experimental.pallas import tpu as pltpu
from jax.sharding import PartitionSpec as P

MESH = pl.DeviceIdType.MESH
LANES = 128
BLOCK = 256
CHUNKS = 2


def layer_kernel(
    n,
    tokens_hbm,
    value_hbm,
    gate_hbm,
    out_hbm,
    head_hbm,
    bias_hbm,
    mixed_ref,
    tokens,
    value_w,
    gate_w,
    out_w,
    head_w,
    bias,
    outgoing,
    held,
    lag_send,
    lags,
    band,
    open_gate,
    result,
    returned,
    total,
    load_sems,
    entry_sems,
    lag_sems,
    sems,
):
    rows, model = tokens.shape
    heads = head_w.shape[0]
    chunks, _, wide, _ = outgoing.shape
    width = chunks * wide
    length = n * rows
    per = BLOCK // width
    blocks = n // per
    half = blocks // 2
    bits = per.bit_length() - 1
    share = n // heads
    me = lax.axis_index("seq")
    mine = me // per
    inside = lax.rem(me, per)
    lower = mine < half
    depth = jnp.where(lower, mine, blocks - 1 - mine)
    inward = jnp.where(lower, me + per, me - per)
    outward = jnp.where(lower, me - per, me + per)
    innermost = depth == half - 1
    outermost = depth == 0

    def place(off):
        ahead = half + off if off < half else lax.rem(depth + 1 + off - half, half)
        return jnp.where(lower, ahead, blocks - 1 - ahead)

    def load(source, target, slot):
        return pltpu.make_async_copy(source, target, load_sems.at[slot])

    def value_load(off):
        columns = pl.ds(pl.multiple_of(place(off) * BLOCK, BLOCK), BLOCK)
        return load(value_hbm.at[:, columns], value_w.at[off], 5 + off)

    tokens_load = load(tokens_hbm, tokens, 0)
    gate_load = load(gate_hbm, gate_w, 1)
    out_load = load(out_hbm, out_w, 2)
    head_load = load(head_hbm, head_w, 3)
    bias_load = load(bias_hbm, bias, 4)
    barrier = pltpu.get_barrier_semaphore()

    def signal(semaphore, peer):
        pl.semaphore_signal(semaphore, inc=1, device_id={"seq": peer}, device_id_type=MESH)

    def loop(action):
        def run(step, carry):
            action(step)
            return carry

        lax.fori_loop(1, n, run, 0)

    @pl.when(innermost)
    def _():
        signal(barrier, inward)

    for bit in range(bits):
        signal(barrier, me ^ (1 << bit))

    @pl.when(jnp.logical_not(outermost))
    def _():
        signal(barrier, outward)

    tokens_load.start()
    value_load(0).start()

    def lag_copy(step):
        peer = lax.rem(me + step, n)
        return pltpu.make_async_remote_copy(
            src_ref=lag_send.at[peer // share],
            dst_ref=lags.at[me],
            send_sem=lag_sems.at[0, step],
            recv_sem=lag_sems.at[1, step],
            device_id={"seq": peer},
            device_id_type=MESH,
        )

    def remote(kind, source, target, chunk, step):
        peer = lax.rem(me + step, n)
        return pltpu.make_async_remote_copy(
            src_ref=source.at[chunk, peer],
            dst_ref=target.at[chunk, me],
            send_sem=sems.at[2 * kind, chunk, step],
            recv_sem=sems.at[2 * kind + 1, chunk, step],
            device_id={"seq": peer},
            device_id_type=MESH,
        )

    def value_copy(chunk, step):
        return remote(0, outgoing, held, chunk, step)

    def back_copy(chunk, step):
        return remote(1, result, returned, chunk, step)

    def send_block(off, chunk, make, first=0, last=per):
        for turn in range(max(first, 1) if off == blocks - 1 else first, last):
            peer = place(off) * per + lax.rem(inside + turn, per)
            make(chunk, lax.rem(peer - me + n, n)).start()

    def project(off):
        value_load(off).wait()
        block = jnp.dot(tokens[...], value_w[off], preferred_element_type=jnp.float32)
        block = block.astype(jnp.bfloat16).T.reshape(per, chunks, wide, rows)
        for chunk in range(chunks):
            outgoing[chunk, pl.ds(place(off) * per, per)] = block[:, chunk]

    def swap(bit):
        signal(entry_sems.at[bit], me ^ (1 << bit))

    def swapped(bit):
        pl.semaphore_wait(entry_sems.at[bit], 1)

    def gather():
        @pl.when(jnp.logical_not(outermost))
        def _():
            pl.semaphore_wait(entry_sems.at[bits], 1)

        @pl.when(innermost)
        def _():
            signal(entry_sems.at[bits + 1], inward)

        @pl.when(jnp.logical_not(innermost | outermost))
        def _():
            signal(entry_sems.at[bits], inward)

    def spread():
        pl.semaphore_wait(entry_sems.at[bits + 1], 1)

        @pl.when(jnp.logical_not(outermost))
        def _():
            signal(entry_sems.at[bits + 1], outward)

    pl.semaphore_wait(barrier, bits + 1)
    for bit in range(min(bits, 1)):
        swap(bit)
    tokens_load.wait()
    project(0)
    for off in range(1, blocks):
        value_load(off).start()
    head_load.start()
    bias_load.start()

    @pl.when(innermost)
    def _():
        send_block(0, 0, value_copy, 0, 1)

    for bit in range(bits):
        if bit > 0:
            swap(bit)
        swapped(bit)

    @pl.when(outermost & jnp.logical_not(innermost))
    def _():
        signal(entry_sems.at[bits], inward)

    @pl.when(innermost)
    def _():
        send_block(0, 0, value_copy, 1, per)

    known = min(2, blocks - 1)
    for off in range(1, blocks):
        project(off)
        if off == 1:
            gate_load.start()
            out_load.start()
            gather()
        if off == known:
            head_load.wait()
            bias_load.wait()
            logits = lax.dot_general(
                head_w[...], tokens[...], (((1,), (1,)), ((), ())), preferred_element_type=jnp.float32
            )
            across = lax.broadcasted_iota(jnp.int32, (heads, heads), 1)
            down = lax.broadcasted_iota(jnp.int32, (heads, heads), 0)
            column = jnp.where(across == down, jnp.broadcast_to(bias[...], (heads, heads)), 0.0)
            column = jnp.sum(column, axis=1, keepdims=True)
            made = jnp.tanh(logits + column) * length ** (-0.5)
            for head in range(heads):
                pieces = [
                    made[head : head + 1, start : start + LANES] for start in range(0, rows, LANES)
                ]
                lag_send[head] = jnp.concatenate(pieces, axis=0).astype(jnp.bfloat16)
            spread()

            @pl.when(jnp.logical_not(innermost))
            def _():
                send_block(0, 0, value_copy)

            for earlier in range(1, off + 1):
                send_block(earlier, 0, value_copy)
            loop(lambda step: lag_copy(step).start())
            lags[me] = lag_send[me // share]
        elif off > known:
            send_block(off, 0, value_copy)
    for chunk in range(1, chunks):
        for off in range(blocks):
            send_block(off, chunk, value_copy)
    for chunk in range(chunks):
        held[chunk, me] = outgoing[chunk, me]

    gate_load.wait()
    for part in range(model // BLOCK):
        gate = jnp.dot(
            tokens[...], gate_w[:, part * BLOCK : (part + 1) * BLOCK], preferred_element_type=jnp.float32
        )
        gate = (gate / (1.0 + jnp.exp(-gate))).T.reshape(per, chunks, wide, rows)
        for chunk in range(chunks):
            open_gate[chunk, part * per : (part + 1) * per] = gate[:, chunk]

    loop(lambda step: lag_copy(step).wait())
    pieces = []
    for source in range(n):
        lag = lags[source].astype(jnp.float32)
        pieces += [lag[index : index + 1] for index in range(rows // LANES)]
    row = jnp.concatenate(pieces[-(rows // LANES) - 1 :] + pieces, axis=1)
    for start in range(0, length + rows, rows):
        piece = jnp.broadcast_to(row[:, start : start + rows + LANES], (LANES, rows + LANES))
        turned = pltpu.roll(piece, 0, 1, stride=1, stride_axis=0)[:, LANES:]
        band[:, start : start + rows] = turned.astype(jnp.bfloat16)

    part = n // 2
    group = min(part, max(1, BLOCK // wide))
    reach = min(n, 16)

    def convolve(chunk, carry):
        loop(lambda step: value_copy(chunk, step).wait())
        held[chunk, n : 2 * n] = held[chunk, 0:n]
        for far in range(2):
            base = jnp.where(lower == (far == 0), part, 0)

            def outputs(index, inner):
                first = base + index * group
                summed = None
                for start in range(0, n, reach):
                    left = jnp.concatenate(
                        [
                            held[chunk, pl.ds(first + at, group)].reshape(group * wide, rows)
                            for at in range(start, start + reach)
                        ],
                        axis=1,
                    )
                    right = jnp.concatenate(
                        [
                            band[:, pl.ds((rows - at) if at <= rows else length + rows - at, rows)]
                            for at in range(start * rows, (start + reach) * rows, LANES)
                        ],
                        axis=0,
                    )
                    term = jnp.dot(left, right, preferred_element_type=jnp.float32)
                    summed = term if summed is None else summed + term
                result[chunk, pl.ds(first, group)] = summed.astype(jnp.bfloat16).reshape(group, wide, rows)
                return inner

            lax.fori_loop(0, part // group, outputs, 0)
            for off in reversed(range(half)) if far == 0 else range(half, blocks):
                send_block(off, chunk, back_copy)
        returned[chunk, me] = result[chunk, me]
        return carry

    lax.fori_loop(0, chunks, convolve, 0)

    out_load.wait()
    for chunk in range(chunks):
        for far in range(2):
            base = jnp.where(lower == (far == 0), 0, part)

            def arrive(index, carry):
                step = lax.rem(me - (base + index) + n, n)

                @pl.when(step > 0)
                def _():
                    back_copy(chunk, step).wait_recv()

                return carry

            lax.fori_loop(0, part, arrive, 0)
            chosen = pl.ds(base, part)
            gated = returned[chunk, chosen].astype(jnp.float32) * open_gate[chunk, chosen]
            gated = gated.astype(jnp.bfloat16).reshape(part * wide, rows).T
            weight = out_w[chosen, chunk].reshape(part * wide, model)
            term = jnp.dot(gated, weight, preferred_element_type=jnp.float32)
            if chunk + far > 0:
                term = total[...] + term
            if chunk + far < chunks:
                total[...] = term
            else:
                mixed_ref[...] = term.astype(jnp.bfloat16)
    for chunk in range(chunks):
        loop(lambda step: back_copy(chunk, step).wait_send())


def body(tokens, value_weight, gate_weight, out_weight, kernel_weight, kernel_bias):
    rows, model = tokens.shape
    heads = kernel_weight.shape[1]
    n = lax.axis_size("seq")
    width = model // n
    chunks = max(1, min(CHUNKS, width // 16))
    wide = width // chunks
    length = rows * n
    per = BLOCK // width
    half = jnp.bfloat16
    operands = (
        tokens,
        value_weight,
        gate_weight,
        out_weight.reshape(n, chunks, wide, model),
        kernel_weight.T,
        kernel_bias.reshape(1, heads),
    )
    return pl.pallas_call(
        functools.partial(layer_kernel, n),
        out_shape=pltpu.VMEM((rows, model), half),
        in_specs=[pl.BlockSpec(memory_space=pl.ANY)] * len(operands),
        out_specs=pl.BlockSpec(memory_space=pltpu.VMEM),
        scratch_shapes=[
            pltpu.VMEM((rows, model), half),
            pltpu.VMEM((n // per, model, BLOCK), half),
            pltpu.VMEM((model, model), half),
            pltpu.VMEM((n, chunks, wide, model), half),
            pltpu.VMEM((heads, model), half),
            pltpu.VMEM((1, heads), jnp.float32),
            pltpu.VMEM((chunks, n, wide, rows), half),
            pltpu.VMEM((chunks, 2 * n, wide, rows), half),
            pltpu.VMEM((heads, rows // LANES, LANES), half),
            pltpu.VMEM((n, rows // LANES, LANES), half),
            pltpu.VMEM((LANES, length + rows), half),
            pltpu.VMEM((chunks, n, wide, rows), jnp.float32),
            pltpu.VMEM((chunks, n, wide, rows), half),
            pltpu.VMEM((chunks, n, wide, rows), half),
            pltpu.VMEM((rows, model), jnp.float32),
            pltpu.SemaphoreType.DMA((5 + n // per,)),
            pltpu.SemaphoreType.REGULAR((per.bit_length() + 1,)),
            pltpu.SemaphoreType.DMA((2, n)),
            pltpu.SemaphoreType.DMA((4, chunks, n)),
        ],
        compiler_params=pltpu.CompilerParams(
            collective_id=0, has_side_effects=True, vmem_limit_bytes=48 * 2**20
        ),
    )(*[pltpu.with_memory_space_constraint(operand, pltpu.HBM) for operand in operands])


def solution(mesh):
    placed = (P(("grp", "seq"), None), P(), P(), P(), P(), P())
    return jax.shard_map(
        body, mesh=mesh, in_specs=placed, out_specs=P(("grp", "seq"), None), check_vma=False
    )
```

```python
import functools

import jax
import jax.numpy as jnp
from jax import lax
from jax.experimental import pallas as pl
from jax.experimental.pallas import tpu as pltpu
from jax.sharding import PartitionSpec as P

MESH = pl.DeviceIdType.MESH
LANES = 128
BLOCK = 256
CHUNKS = 2


def layer_kernel(
    n,
    tokens_hbm,
    value_hbm,
    gate_hbm,
    out_hbm,
    head_hbm,
    bias_hbm,
    mixed_ref,
    tokens,
    value_w,
    gate_w,
    out_w,
    head_w,
    bias,
    outgoing,
    held,
    lag_send,
    lags,
    band,
    open_gate,
    result,
    returned,
    total,
    load_sems,
    entry_sems,
    lag_sems,
    sems,
):
    rows, model = tokens.shape
    heads = head_w.shape[0]
    chunks, _, wide, _ = outgoing.shape
    width = chunks * wide
    length = n * rows
    per = BLOCK // width
    blocks = n // per
    half = blocks // 2
    bits = per.bit_length() - 1
    share = n // heads
    me = lax.axis_index("seq")
    mine = me // per
    inside = lax.rem(me, per)
    lower = mine < half
    depth = jnp.where(lower, mine, blocks - 1 - mine)
    inward = jnp.where(lower, me + per, me - per)
    outward = jnp.where(lower, me - per, me + per)
    innermost = depth == half - 1
    outermost = depth == 0

    def place(off):
        ahead = half + off if off < half else lax.rem(depth + 1 + off - half, half)
        return jnp.where(lower, ahead, blocks - 1 - ahead)

    def load(source, target, slot):
        return pltpu.make_async_copy(source, target, load_sems.at[slot])

    def value_load(off):
        columns = pl.ds(pl.multiple_of(place(off) * BLOCK, BLOCK), BLOCK)
        return load(value_hbm.at[:, columns], value_w.at[off], 5 + off)

    tokens_load = load(tokens_hbm, tokens, 0)
    gate_load = load(gate_hbm, gate_w, 1)
    out_load = load(out_hbm, out_w, 2)
    head_load = load(head_hbm, head_w, 3)
    bias_load = load(bias_hbm, bias, 4)
    barrier = pltpu.get_barrier_semaphore()

    def signal(semaphore, peer):
        pl.semaphore_signal(semaphore, inc=1, device_id={"seq": peer}, device_id_type=MESH)

    def loop(action):
        def run(step, carry):
            action(step)
            return carry

        lax.fori_loop(1, n, run, 0)

    @pl.when(innermost)
    def _():
        signal(barrier, inward)

    for bit in range(bits):
        signal(barrier, me ^ (1 << bit))

    @pl.when(jnp.logical_not(outermost))
    def _():
        signal(barrier, outward)

    tokens_load.start()
    value_load(0).start()

    def lag_copy(step):
        peer = lax.rem(me + step, n)
        return pltpu.make_async_remote_copy(
            src_ref=lag_send.at[peer // share],
            dst_ref=lags.at[me],
            send_sem=lag_sems.at[0],
            recv_sem=lag_sems.at[1],
            device_id={"seq": peer},
            device_id_type=MESH,
        )

    def remote(source, target, chunk, step, sent, received):
        peer = lax.rem(me + step, n)
        return pltpu.make_async_remote_copy(
            src_ref=source.at[chunk, peer],
            dst_ref=target.at[chunk, me],
            send_sem=sems.at[sent],
            recv_sem=sems.at[received],
            device_id={"seq": peer},
            device_id_type=MESH,
        )

    def value_copy(chunk, step):
        return remote(outgoing, held, chunk, step, 0, 2 + chunk)

    def back_copy(chunk, step):
        near = (lax.rem(me + step, n) < half * per) == lower
        return remote(result, returned, chunk, step, 1, 2 + chunks + 2 * chunk + jnp.where(near, 0, 1))

    def finish(slots, semaphore):
        pltpu.make_async_copy(slots, slots, semaphore).wait()

    def send_block(off, chunk, make, first=0, last=per):
        for turn in range(max(first, 1) if off == blocks - 1 else first, last):
            peer = place(off) * per + lax.rem(inside + turn, per)
            make(chunk, lax.rem(peer - me + n, n)).start()

    def project(off):
        value_load(off).wait()
        block = jnp.dot(tokens[...], value_w[off], preferred_element_type=jnp.float32)
        block = block.astype(jnp.bfloat16).T.reshape(per, chunks, wide, rows)
        for chunk in range(chunks):
            outgoing[chunk, pl.ds(place(off) * per, per)] = block[:, chunk]

    def swap(bit):
        signal(entry_sems.at[bit], me ^ (1 << bit))

    def swapped(bit):
        pl.semaphore_wait(entry_sems.at[bit], 1)

    def gather():
        @pl.when(jnp.logical_not(outermost))
        def _():
            pl.semaphore_wait(entry_sems.at[bits], 1)

        @pl.when(innermost)
        def _():
            signal(entry_sems.at[bits + 1], inward)

        @pl.when(jnp.logical_not(innermost | outermost))
        def _():
            signal(entry_sems.at[bits], inward)

    def spread():
        pl.semaphore_wait(entry_sems.at[bits + 1], 1)

        @pl.when(jnp.logical_not(outermost))
        def _():
            signal(entry_sems.at[bits + 1], outward)

    pl.semaphore_wait(barrier, bits + 1)
    for bit in range(min(bits, 1)):
        swap(bit)
    tokens_load.wait()
    project(0)
    for off in range(1, blocks):
        value_load(off).start()
    head_load.start()
    bias_load.start()

    @pl.when(innermost)
    def _():
        for chunk in range(chunks):
            send_block(0, chunk, value_copy, 0, 1)

    for bit in range(bits):
        if bit > 0:
            swap(bit)
        swapped(bit)

    @pl.when(outermost & jnp.logical_not(innermost))
    def _():
        signal(entry_sems.at[bits], inward)

    @pl.when(innermost)
    def _():
        send_block(0, 0, value_copy, 1, per)

    known = min(2, blocks - 1)
    for off in range(1, blocks):
        project(off)
        if off == 1:
            gate_load.start()
            out_load.start()
            gather()
        if off == known:
            head_load.wait()
            bias_load.wait()
            logits = lax.dot_general(
                head_w[...], tokens[...], (((1,), (1,)), ((), ())), preferred_element_type=jnp.float32
            )
            across = lax.broadcasted_iota(jnp.int32, (heads, heads), 1)
            down = lax.broadcasted_iota(jnp.int32, (heads, heads), 0)
            column = jnp.where(across == down, jnp.broadcast_to(bias[...], (heads, heads)), 0.0)
            column = jnp.sum(column, axis=1, keepdims=True)
            made = jnp.tanh(logits + column) * length ** (-0.5)
            for head in range(heads):
                pieces = [
                    made[head : head + 1, start : start + LANES] for start in range(0, rows, LANES)
                ]
                lag_send[head] = jnp.concatenate(pieces, axis=0).astype(jnp.bfloat16)
            spread()

            @pl.when(jnp.logical_not(innermost))
            def _():
                send_block(0, 0, value_copy)

            for earlier in range(1, off + 1):
                send_block(earlier, 0, value_copy)
            loop(lambda step: lag_copy(step).start())
            lags[me] = lag_send[me // share]
        elif off > known:
            send_block(off, 0, value_copy)
    for chunk in range(1, chunks):
        pl.when(jnp.logical_not(innermost))(functools.partial(send_block, 0, chunk, value_copy, 0, 1))
        send_block(0, chunk, value_copy, 1, per)
        for off in range(1, blocks):
            send_block(off, chunk, value_copy)
    for chunk in range(chunks):
        held[chunk, me] = outgoing[chunk, me]

    gate_load.wait()
    for part in range(model // BLOCK):
        gate = jnp.dot(
            tokens[...], gate_w[:, part * BLOCK : (part + 1) * BLOCK], preferred_element_type=jnp.float32
        )
        gate = (gate / (1.0 + jnp.exp(-gate))).T.reshape(per, chunks, wide, rows)
        for chunk in range(chunks):
            open_gate[chunk, part * per : (part + 1) * per] = gate[:, chunk]

    finish(lags.at[pl.ds(0, n - 1)], lag_sems.at[1])
    pieces = []
    for source in range(n):
        lag = lags[source].astype(jnp.float32)
        pieces += [lag[index : index + 1] for index in range(rows // LANES)]
    row = jnp.concatenate(pieces[-(rows // LANES) - 1 :] + pieces, axis=1)
    for start in range(0, length + rows, rows):
        piece = jnp.broadcast_to(row[:, start : start + rows + LANES], (LANES, rows + LANES))
        turned = pltpu.roll(piece, 0, 1, stride=1, stride_axis=0)[:, LANES:]
        band[:, start : start + rows] = turned.astype(jnp.bfloat16)

    part = n // 2
    group = min(part, max(1, BLOCK // wide))
    reach = min(n, 16)

    def convolve(chunk, carry):
        finish(held.at[chunk, pl.ds(0, n - 1)], sems.at[2 + chunk])
        held[chunk, n : 2 * n] = held[chunk, 0:n]
        for far in range(2):
            base = jnp.where(lower == (far == 0), part, 0)

            def outputs(index, inner):
                first = base + index * group
                summed = None
                for start in range(0, n, reach):
                    left = jnp.concatenate(
                        [
                            held[chunk, pl.ds(first + at, group)].reshape(group * wide, rows)
                            for at in range(start, start + reach)
                        ],
                        axis=1,
                    )
                    right = jnp.concatenate(
                        [
                            band[:, pl.ds((rows - at) if at <= rows else length + rows - at, rows)]
                            for at in range(start * rows, (start + reach) * rows, LANES)
                        ],
                        axis=0,
                    )
                    term = jnp.dot(left, right, preferred_element_type=jnp.float32)
                    summed = term if summed is None else summed + term
                result[chunk, pl.ds(first, group)] = summed.astype(jnp.bfloat16).reshape(group, wide, rows)
                return inner

            lax.fori_loop(0, part // group, outputs, 0)
            for off in reversed(range(half)) if far == 0 else range(half, blocks):
                send_block(off, chunk, back_copy)
        returned[chunk, me] = result[chunk, me]
        return carry

    lax.fori_loop(0, chunks, convolve, 0)

    out_load.wait()
    for chunk in range(chunks):
        for far in range(2):
            base = jnp.where(lower == (far == 0), 0, part)

            finish(returned.at[chunk, pl.ds(0, part - 1 + far)], sems.at[2 + chunks + 2 * chunk + far])
            chosen = pl.ds(base, part)
            gated = returned[chunk, chosen].astype(jnp.float32) * open_gate[chunk, chosen]
            gated = gated.astype(jnp.bfloat16).reshape(part * wide, rows).T
            weight = out_w[chosen, chunk].reshape(part * wide, model)
            term = jnp.dot(gated, weight, preferred_element_type=jnp.float32)
            if chunk + far > 0:
                term = total[...] + term
            if chunk + far < chunks:
                total[...] = term
            else:
                mixed_ref[...] = term.astype(jnp.bfloat16)
    finish(lags.at[pl.ds(0, n - 1)], lag_sems.at[0])
    for sent in range(2):
        finish(returned.at[:, pl.ds(0, n - 1)], sems.at[sent])


def body(tokens, value_weight, gate_weight, out_weight, kernel_weight, kernel_bias):
    rows, model = tokens.shape
    heads = kernel_weight.shape[1]
    n = lax.axis_size("seq")
    width = model // n
    chunks = max(1, min(CHUNKS, width // 16))
    wide = width // chunks
    length = rows * n
    per = BLOCK // width
    half = jnp.bfloat16
    operands = (
        tokens,
        value_weight,
        gate_weight,
        out_weight.reshape(n, chunks, wide, model),
        kernel_weight.T,
        kernel_bias.reshape(1, heads),
    )
    return pl.pallas_call(
        functools.partial(layer_kernel, n),
        out_shape=pltpu.VMEM((rows, model), half),
        in_specs=[pl.BlockSpec(memory_space=pl.ANY)] * len(operands),
        out_specs=pl.BlockSpec(memory_space=pltpu.VMEM),
        scratch_shapes=[
            pltpu.VMEM((rows, model), half),
            pltpu.VMEM((n // per, model, BLOCK), half),
            pltpu.VMEM((model, model), half),
            pltpu.VMEM((n, chunks, wide, model), half),
            pltpu.VMEM((heads, model), half),
            pltpu.VMEM((1, heads), jnp.float32),
            pltpu.VMEM((chunks, n, wide, rows), half),
            pltpu.VMEM((chunks, 2 * n, wide, rows), half),
            pltpu.VMEM((heads, rows // LANES, LANES), half),
            pltpu.VMEM((n, rows // LANES, LANES), half),
            pltpu.VMEM((LANES, length + rows), half),
            pltpu.VMEM((chunks, n, wide, rows), jnp.float32),
            pltpu.VMEM((chunks, n, wide, rows), half),
            pltpu.VMEM((chunks, n, wide, rows), half),
            pltpu.VMEM((rows, model), jnp.float32),
            pltpu.SemaphoreType.DMA((5 + n // per,)),
            pltpu.SemaphoreType.REGULAR((per.bit_length() + 1,)),
            pltpu.SemaphoreType.DMA((2,)),
            pltpu.SemaphoreType.DMA((2 + 3 * chunks,)),
        ],
        compiler_params=pltpu.CompilerParams(
            collective_id=0, has_side_effects=True, vmem_limit_bytes=48 * 2**20
        ),
    )(*[pltpu.with_memory_space_constraint(operand, pltpu.HBM) for operand in operands])


def solution(mesh):
    placed = (P(("grp", "seq"), None), P(), P(), P(), P(), P())
    return jax.shard_map(
        body, mesh=mesh, in_specs=placed, out_specs=P(("grp", "seq"), None), check_vma=False
    )
```

```python
import functools

import jax
import jax.numpy as jnp
from jax import lax
from jax.experimental import pallas as pl
from jax.experimental.pallas import tpu as pltpu
from jax.sharding import PartitionSpec as P

MESH = pl.DeviceIdType.MESH
LANES = 128
BLOCK = 256
CHUNKS = 2


def layer_kernel(
    n,
    tokens_hbm,
    value_hbm,
    gate_hbm,
    out_hbm,
    head_hbm,
    bias_hbm,
    mixed_ref,
    tokens,
    value_w,
    gate_w,
    out_w,
    head_w,
    bias,
    outgoing,
    held,
    lag_send,
    lags,
    band,
    open_gate,
    result,
    returned,
    total,
    load_sems,
    entry_sems,
    lag_sems,
    sems,
):
    rows, model = tokens.shape
    heads = head_w.shape[0]
    chunks, _, wide, _ = outgoing.shape
    width = chunks * wide
    length = n * rows
    per = BLOCK // width
    blocks = n // per
    half = blocks // 2
    bits = per.bit_length() - 1
    share = n // heads
    me = lax.axis_index("seq")
    mine = me // per
    inside = lax.rem(me, per)
    lower = mine < half
    depth = jnp.where(lower, mine, blocks - 1 - mine)
    inward = jnp.where(lower, me + per, me - per)
    outward = jnp.where(lower, me - per, me + per)
    innermost = depth == half - 1
    outermost = depth == 0

    def place(off):
        ahead = half + off if off < half else lax.rem(depth + 1 + off - half, half)
        return jnp.where(lower, ahead, blocks - 1 - ahead)

    def load(source, target, slot):
        return pltpu.make_async_copy(source, target, load_sems.at[slot])

    def value_load(off):
        columns = pl.ds(pl.multiple_of(place(off) * BLOCK, BLOCK), BLOCK)
        return load(value_hbm.at[:, columns], value_w.at[off], 5 + off)

    tokens_load = load(tokens_hbm, tokens, 0)
    gate_load = load(gate_hbm, gate_w, 1)
    out_load = load(out_hbm, out_w, 2)
    head_load = load(head_hbm, head_w, 3)
    bias_load = load(bias_hbm, bias, 4)
    barrier = pltpu.get_barrier_semaphore()

    def signal(semaphore, peer):
        pl.semaphore_signal(semaphore, inc=1, device_id={"seq": peer}, device_id_type=MESH)

    def loop(action):
        def run(step, carry):
            action(step)
            return carry

        lax.fori_loop(1, n, run, 0)

    @pl.when(innermost)
    def _():
        signal(barrier, inward)

    for bit in range(bits):
        signal(barrier, me ^ (1 << bit))

    @pl.when(jnp.logical_not(outermost))
    def _():
        signal(barrier, outward)

    tokens_load.start()
    value_load(0).start()

    def lag_copy(step):
        peer = lax.rem(me + step, n)
        return pltpu.make_async_remote_copy(
            src_ref=lag_send.at[peer // share],
            dst_ref=lags.at[me],
            send_sem=lag_sems.at[0],
            recv_sem=lag_sems.at[1],
            device_id={"seq": peer},
            device_id_type=MESH,
        )

    def remote(source, target, chunk, step, sent, received):
        peer = lax.rem(me + step, n)
        return pltpu.make_async_remote_copy(
            src_ref=source.at[chunk, peer],
            dst_ref=target.at[chunk, me],
            send_sem=sems.at[sent],
            recv_sem=sems.at[received],
            device_id={"seq": peer},
            device_id_type=MESH,
        )

    def value_copy(chunk, step):
        return remote(outgoing, held, chunk, step, 0, 2 + chunk)

    def back_copy(chunk, step):
        near = (lax.rem(me + step, n) < half * per) == lower
        return remote(result, returned, chunk, step, 1, 2 + chunks + 2 * chunk + jnp.where(near, 0, 1))

    def finish(slots, semaphore):
        pltpu.make_async_copy(slots, slots, semaphore).wait()

    def send_block(off, chunk, make, first=0, last=per):
        for turn in range(max(first, 1) if off == blocks - 1 else first, last):
            peer = place(off) * per + lax.rem(inside + turn, per)
            make(chunk, lax.rem(peer - me + n, n)).start()

    def project(off):
        value_load(off).wait()
        block = jnp.dot(tokens[...], value_w[off], preferred_element_type=jnp.float32)
        block = block.astype(jnp.bfloat16).T.reshape(per, chunks, wide, rows)
        for chunk in range(chunks):
            outgoing[chunk, pl.ds(place(off) * per, per)] = block[:, chunk]

    def swap(bit):
        signal(entry_sems.at[bit], me ^ (1 << bit))

    def swapped(bit):
        pl.semaphore_wait(entry_sems.at[bit], 1)

    def gather():
        @pl.when(jnp.logical_not(outermost))
        def _():
            pl.semaphore_wait(entry_sems.at[bits], 1)

        @pl.when(innermost)
        def _():
            signal(entry_sems.at[bits + 1], inward)

        @pl.when(jnp.logical_not(innermost | outermost))
        def _():
            signal(entry_sems.at[bits], inward)

    def spread():
        pl.semaphore_wait(entry_sems.at[bits + 1], 1)

        @pl.when(jnp.logical_not(outermost))
        def _():
            signal(entry_sems.at[bits + 1], outward)

    pl.semaphore_wait(barrier, bits + 1)
    for bit in range(min(bits, 1)):
        swap(bit)
    tokens_load.wait()
    project(0)
    for off in range(1, blocks):
        value_load(off).start()
    head_load.start()
    bias_load.start()

    @pl.when(innermost)
    def _():
        for chunk in range(chunks):
            send_block(0, chunk, value_copy, 0, 1)

    for bit in range(bits):
        if bit > 0:
            swap(bit)
        swapped(bit)

    @pl.when(outermost & jnp.logical_not(innermost))
    def _():
        signal(entry_sems.at[bits], inward)

    @pl.when(innermost)
    def _():
        send_block(0, 0, value_copy, 1, per)

    gather()
    known = min(1, blocks - 1)
    for off in range(1, blocks):
        project(off)
        if off == 1:
            gate_load.start()
            out_load.start()
        if off == known:
            spread()

            @pl.when(jnp.logical_not(innermost))
            def _():
                send_block(0, 0, value_copy)

            for earlier in range(1, off + 1):
                send_block(earlier, 0, value_copy)
            head_load.wait()
            bias_load.wait()
            logits = lax.dot_general(
                head_w[...], tokens[...], (((1,), (1,)), ((), ())), preferred_element_type=jnp.float32
            )
            across = lax.broadcasted_iota(jnp.int32, (heads, heads), 1)
            down = lax.broadcasted_iota(jnp.int32, (heads, heads), 0)
            column = jnp.where(across == down, jnp.broadcast_to(bias[...], (heads, heads)), 0.0)
            column = jnp.sum(column, axis=1, keepdims=True)
            made = jnp.tanh(logits + column) * length ** (-0.5)
            for head in range(heads):
                pieces = [
                    made[head : head + 1, start : start + LANES] for start in range(0, rows, LANES)
                ]
                lag_send[head] = jnp.concatenate(pieces, axis=0).astype(jnp.bfloat16)
            loop(lambda step: lag_copy(step).start())
            lags[me] = lag_send[me // share]
        elif off > known:
            send_block(off, 0, value_copy)
    for chunk in range(1, chunks):
        pl.when(jnp.logical_not(innermost))(functools.partial(send_block, 0, chunk, value_copy, 0, 1))
        send_block(0, chunk, value_copy, 1, per)
        for off in range(1, blocks):
            send_block(off, chunk, value_copy)
    for chunk in range(chunks):
        held[chunk, me] = outgoing[chunk, me]

    gate_load.wait()
    for part in range(model // BLOCK):
        gate = jnp.dot(
            tokens[...], gate_w[:, part * BLOCK : (part + 1) * BLOCK], preferred_element_type=jnp.float32
        )
        gate = (gate / (1.0 + jnp.exp(-gate))).T.reshape(per, chunks, wide, rows)
        for chunk in range(chunks):
            open_gate[chunk, part * per : (part + 1) * per] = gate[:, chunk]

    finish(lags.at[pl.ds(0, n - 1)], lag_sems.at[1])
    pieces = []
    for source in range(n):
        lag = lags[source].astype(jnp.float32)
        pieces += [lag[index : index + 1] for index in range(rows // LANES)]
    row = jnp.concatenate(pieces[-(rows // LANES) - 1 :] + pieces, axis=1)
    for start in range(0, length + rows, rows):
        piece = jnp.broadcast_to(row[:, start : start + rows + LANES], (LANES, rows + LANES))
        turned = pltpu.roll(piece, 0, 1, stride=1, stride_axis=0)[:, LANES:]
        band[:, start : start + rows] = turned.astype(jnp.bfloat16)

    part = n // 2
    group = min(part, max(1, BLOCK // wide))
    reach = min(n, 16)

    def convolve(chunk, carry):
        finish(held.at[chunk, pl.ds(0, n - 1)], sems.at[2 + chunk])
        held[chunk, n : 2 * n] = held[chunk, 0:n]
        for far in range(2):
            base = jnp.where(lower == (far == 0), part, 0)

            def outputs(index, inner):
                first = base + index * group
                summed = None
                for start in range(0, n, reach):
                    left = jnp.concatenate(
                        [
                            held[chunk, pl.ds(first + at, group)].reshape(group * wide, rows)
                            for at in range(start, start + reach)
                        ],
                        axis=1,
                    )
                    right = jnp.concatenate(
                        [
                            band[:, pl.ds((rows - at) if at <= rows else length + rows - at, rows)]
                            for at in range(start * rows, (start + reach) * rows, LANES)
                        ],
                        axis=0,
                    )
                    term = jnp.dot(left, right, preferred_element_type=jnp.float32)
                    summed = term if summed is None else summed + term
                result[chunk, pl.ds(first, group)] = summed.astype(jnp.bfloat16).reshape(group, wide, rows)
                return inner

            lax.fori_loop(0, part // group, outputs, 0)
            for off in reversed(range(half)) if far == 0 else range(half, blocks):
                send_block(off, chunk, back_copy)
        returned[chunk, me] = result[chunk, me]
        return carry

    lax.fori_loop(0, chunks, convolve, 0)

    out_load.wait()
    for chunk in range(chunks):
        for far in range(2):
            base = jnp.where(lower == (far == 0), 0, part)

            finish(returned.at[chunk, pl.ds(0, part - 1 + far)], sems.at[2 + chunks + 2 * chunk + far])
            chosen = pl.ds(base, part)
            gated = returned[chunk, chosen].astype(jnp.float32) * open_gate[chunk, chosen]
            gated = gated.astype(jnp.bfloat16).reshape(part * wide, rows).T
            weight = out_w[chosen, chunk].reshape(part * wide, model)
            term = jnp.dot(gated, weight, preferred_element_type=jnp.float32)
            if chunk + far > 0:
                term = total[...] + term
            if chunk + far < chunks:
                total[...] = term
            else:
                mixed_ref[...] = term.astype(jnp.bfloat16)
    finish(lags.at[pl.ds(0, n - 1)], lag_sems.at[0])
    for sent in range(2):
        finish(returned.at[:, pl.ds(0, n - 1)], sems.at[sent])


def body(tokens, value_weight, gate_weight, out_weight, kernel_weight, kernel_bias):
    rows, model = tokens.shape
    heads = kernel_weight.shape[1]
    n = lax.axis_size("seq")
    width = model // n
    chunks = max(1, min(CHUNKS, width // 16))
    wide = width // chunks
    length = rows * n
    per = BLOCK // width
    half = jnp.bfloat16
    operands = (
        tokens,
        value_weight,
        gate_weight,
        out_weight.reshape(n, chunks, wide, model),
        kernel_weight.T,
        kernel_bias.reshape(1, heads),
    )
    return pl.pallas_call(
        functools.partial(layer_kernel, n),
        out_shape=pltpu.VMEM((rows, model), half),
        in_specs=[pl.BlockSpec(memory_space=pl.ANY)] * len(operands),
        out_specs=pl.BlockSpec(memory_space=pltpu.VMEM),
        scratch_shapes=[
            pltpu.VMEM((rows, model), half),
            pltpu.VMEM((n // per, model, BLOCK), half),
            pltpu.VMEM((model, model), half),
            pltpu.VMEM((n, chunks, wide, model), half),
            pltpu.VMEM((heads, model), half),
            pltpu.VMEM((1, heads), jnp.float32),
            pltpu.VMEM((chunks, n, wide, rows), half),
            pltpu.VMEM((chunks, 2 * n, wide, rows), half),
            pltpu.VMEM((heads, rows // LANES, LANES), half),
            pltpu.VMEM((n, rows // LANES, LANES), half),
            pltpu.VMEM((LANES, length + rows), half),
            pltpu.VMEM((chunks, n, wide, rows), jnp.float32),
            pltpu.VMEM((chunks, n, wide, rows), half),
            pltpu.VMEM((chunks, n, wide, rows), half),
            pltpu.VMEM((rows, model), jnp.float32),
            pltpu.SemaphoreType.DMA((5 + n // per,)),
            pltpu.SemaphoreType.REGULAR((per.bit_length() + 1,)),
            pltpu.SemaphoreType.DMA((2,)),
            pltpu.SemaphoreType.DMA((2 + 3 * chunks,)),
        ],
        compiler_params=pltpu.CompilerParams(
            collective_id=0, has_side_effects=True, vmem_limit_bytes=48 * 2**20
        ),
    )(*[pltpu.with_memory_space_constraint(operand, pltpu.HBM) for operand in operands])


def solution(mesh):
    placed = (P(("grp", "seq"), None), P(), P(), P(), P(), P())
    return jax.shard_map(
        body, mesh=mesh, in_specs=placed, out_specs=P(("grp", "seq"), None), check_vma=False
    )
```

```python
import functools

import jax
import jax.numpy as jnp
from jax import lax
from jax.experimental import pallas as pl
from jax.experimental.pallas import tpu as pltpu
from jax.sharding import PartitionSpec as P

MESH = pl.DeviceIdType.MESH
LANES = 128
BLOCK = 256
CHUNKS = 2


def layer_kernel(
    n,
    tokens_hbm,
    value_hbm,
    gate_hbm,
    out_hbm,
    head_hbm,
    bias_hbm,
    mixed_ref,
    tokens,
    value_w,
    gate_w,
    out_w,
    head_w,
    bias,
    outgoing,
    held,
    lag_send,
    lags,
    band,
    open_gate,
    result,
    returned,
    total,
    load_sems,
    entry_sems,
    lag_sems,
    sems,
):
    rows, model = tokens.shape
    heads = head_w.shape[0]
    chunks, _, wide, _ = outgoing.shape
    width = chunks * wide
    length = n * rows
    per = BLOCK // width
    blocks = n // per
    half = blocks // 2
    bits = per.bit_length() - 1
    share = n // heads
    me = lax.axis_index("seq")
    mine = me // per
    inside = lax.rem(me, per)
    lower = mine < half
    depth = jnp.where(lower, mine, blocks - 1 - mine)
    inward = jnp.where(lower, me + per, me - per)
    outward = jnp.where(lower, me - per, me + per)
    innermost = depth == half - 1
    outermost = depth == 0

    def place(off):
        ahead = half + off if off < half else lax.rem(depth + 1 + off - half, half)
        return jnp.where(lower, ahead, blocks - 1 - ahead)

    def load(source, target, slot):
        return pltpu.make_async_copy(source, target, load_sems.at[slot])

    def value_load(off):
        columns = pl.ds(pl.multiple_of(place(off) * BLOCK, BLOCK), BLOCK)
        return load(value_hbm.at[:, columns], value_w.at[off], 3 + off)

    middle = model // 2
    first_loads = []
    for index in range(2):
        deep = pl.ds(index * middle, middle)
        columns = pl.ds(pl.multiple_of(place(0) * BLOCK, BLOCK), BLOCK)
        first_loads.append(
            (
                load(tokens_hbm.at[:, deep], tokens.at[:, deep], 4 + blocks + 2 * index),
                load(value_hbm.at[deep, columns], value_w.at[0, deep], 5 + blocks + 2 * index),
            )
        )
    gate_load = load(gate_hbm, gate_w, 0)
    out_load = load(out_hbm, out_w, 1)
    head_load = load(head_hbm, head_w, 2)
    bias_load = load(bias_hbm, bias, 3)
    barrier = pltpu.get_barrier_semaphore()

    def signal(semaphore, peer):
        pl.semaphore_signal(semaphore, inc=1, device_id={"seq": peer}, device_id_type=MESH)

    def loop(action):
        def run(step, carry):
            action(step)
            return carry

        lax.fori_loop(1, n, run, 0)

    @pl.when(innermost)
    def _():
        signal(barrier, inward)

    for bit in range(bits):
        signal(barrier, me ^ (1 << bit))

    @pl.when(jnp.logical_not(outermost))
    def _():
        signal(barrier, outward)

    for pair in first_loads:
        for part in pair:
            part.start()

    def lag_copy(step):
        peer = lax.rem(me + step, n)
        return pltpu.make_async_remote_copy(
            src_ref=lag_send.at[peer // share],
            dst_ref=lags.at[me],
            send_sem=lag_sems.at[0],
            recv_sem=lag_sems.at[1],
            device_id={"seq": peer},
            device_id_type=MESH,
        )

    def remote(source, target, chunk, step, sent, received):
        peer = lax.rem(me + step, n)
        return pltpu.make_async_remote_copy(
            src_ref=source.at[chunk, peer],
            dst_ref=target.at[chunk, me],
            send_sem=sems.at[sent],
            recv_sem=sems.at[received],
            device_id={"seq": peer},
            device_id_type=MESH,
        )

    def value_copy(chunk, step):
        return remote(outgoing, held, chunk, step, 0, 2 + chunk)

    def back_copy(chunk, step):
        near = (lax.rem(me + step, n) < half * per) == lower
        return remote(result, returned, chunk, step, 1, 2 + chunks + 2 * chunk + jnp.where(near, 0, 1))

    def finish(slots, semaphore):
        pltpu.make_async_copy(slots, slots, semaphore).wait()

    def send_block(off, chunk, make, first=0, last=per):
        for turn in range(max(first, 1) if off == blocks - 1 else first, last):
            peer = place(off) * per + lax.rem(inside + turn, per)
            make(chunk, lax.rem(peer - me + n, n)).start()

    def project(off):
        if off > 0:
            value_load(off).wait()
            block = jnp.dot(tokens[...], value_w[off], preferred_element_type=jnp.float32)
        else:
            block = None
            for index, pair in enumerate(first_loads):
                for part in pair:
                    part.wait()
                deep = slice(index * middle, (index + 1) * middle)
                term = jnp.dot(tokens[:, deep], value_w[0, deep], preferred_element_type=jnp.float32)
                block = term if block is None else block + term
        block = block.astype(jnp.bfloat16).T.reshape(per, chunks, wide, rows)
        for chunk in range(chunks):
            outgoing[chunk, pl.ds(place(off) * per, per)] = block[:, chunk]

    def swap(bit):
        signal(entry_sems.at[bit], me ^ (1 << bit))

    def swapped(bit):
        pl.semaphore_wait(entry_sems.at[bit], 1)

    def gather():
        @pl.when(jnp.logical_not(outermost))
        def _():
            pl.semaphore_wait(entry_sems.at[bits], 1)

        @pl.when(innermost)
        def _():
            signal(entry_sems.at[bits + 1], inward)

        @pl.when(jnp.logical_not(innermost | outermost))
        def _():
            signal(entry_sems.at[bits], inward)

    def spread():
        pl.semaphore_wait(entry_sems.at[bits + 1], 1)

        @pl.when(jnp.logical_not(outermost))
        def _():
            signal(entry_sems.at[bits + 1], outward)

    pl.semaphore_wait(barrier, bits + 1)
    for bit in range(min(bits, 1)):
        swap(bit)
    project(0)
    for off in range(1, blocks):
        value_load(off).start()
    head_load.start()
    bias_load.start()

    @pl.when(innermost)
    def _():
        for chunk in range(chunks):
            send_block(0, chunk, value_copy, 0, 1)

    for bit in range(bits):
        if bit > 0:
            swap(bit)
        swapped(bit)

    @pl.when(outermost & jnp.logical_not(innermost))
    def _():
        signal(entry_sems.at[bits], inward)

    @pl.when(innermost)
    def _():
        send_block(0, 0, value_copy, 1, per)

    gather()
    known = min(1, blocks - 1)
    for off in range(1, blocks):
        project(off)
        if off == 1:
            gate_load.start()
            out_load.start()
        if off == known:
            spread()

            @pl.when(jnp.logical_not(innermost))
            def _():
                send_block(0, 0, value_copy)

            for earlier in range(1, off + 1):
                send_block(earlier, 0, value_copy)
            head_load.wait()
            bias_load.wait()
            logits = lax.dot_general(
                head_w[...], tokens[...], (((1,), (1,)), ((), ())), preferred_element_type=jnp.float32
            )
            across = lax.broadcasted_iota(jnp.int32, (heads, heads), 1)
            down = lax.broadcasted_iota(jnp.int32, (heads, heads), 0)
            column = jnp.where(across == down, jnp.broadcast_to(bias[...], (heads, heads)), 0.0)
            column = jnp.sum(column, axis=1, keepdims=True)
            made = jnp.tanh(logits + column) * length ** (-0.5)
            for head in range(heads):
                pieces = [
                    made[head : head + 1, start : start + LANES] for start in range(0, rows, LANES)
                ]
                lag_send[head] = jnp.concatenate(pieces, axis=0).astype(jnp.bfloat16)
            loop(lambda step: lag_copy(step).start())
            lags[me] = lag_send[me // share]
        elif off > known:
            send_block(off, 0, value_copy)
    for chunk in range(1, chunks):
        pl.when(jnp.logical_not(innermost))(functools.partial(send_block, 0, chunk, value_copy, 0, 1))
        send_block(0, chunk, value_copy, 1, per)
        for off in range(1, blocks):
            send_block(off, chunk, value_copy)
    for chunk in range(chunks):
        held[chunk, me] = outgoing[chunk, me]

    gate_load.wait()
    for part in range(model // BLOCK):
        gate = jnp.dot(
            tokens[...], gate_w[:, part * BLOCK : (part + 1) * BLOCK], preferred_element_type=jnp.float32
        )
        gate = (gate / (1.0 + jnp.exp(-gate))).T.reshape(per, chunks, wide, rows)
        for chunk in range(chunks):
            open_gate[chunk, part * per : (part + 1) * per] = gate[:, chunk]

    finish(lags.at[pl.ds(0, n - 1)], lag_sems.at[1])
    pieces = []
    for source in range(n):
        lag = lags[source].astype(jnp.float32)
        pieces += [lag[index : index + 1] for index in range(rows // LANES)]
    row = jnp.concatenate(pieces[-(rows // LANES) - 1 :] + pieces, axis=1)
    for start in range(0, length + rows, rows):
        piece = jnp.broadcast_to(row[:, start : start + rows + LANES], (LANES, rows + LANES))
        turned = pltpu.roll(piece, 0, 1, stride=1, stride_axis=0)[:, LANES:]
        band[:, start : start + rows] = turned.astype(jnp.bfloat16)

    part = n // 2
    group = min(part, max(1, BLOCK // wide))
    reach = min(n, 16)

    def convolve(chunk, carry):
        finish(held.at[chunk, pl.ds(0, n - 1)], sems.at[2 + chunk])
        held[chunk, n : 2 * n] = held[chunk, 0:n]
        for far in range(2):
            base = jnp.where(lower == (far == 0), part, 0)

            def outputs(index, inner):
                first = base + index * group
                summed = None
                for start in range(0, n, reach):
                    left = jnp.concatenate(
                        [
                            held[chunk, pl.ds(first + at, group)].reshape(group * wide, rows)
                            for at in range(start, start + reach)
                        ],
                        axis=1,
                    )
                    right = jnp.concatenate(
                        [
                            band[:, pl.ds((rows - at) if at <= rows else length + rows - at, rows)]
                            for at in range(start * rows, (start + reach) * rows, LANES)
                        ],
                        axis=0,
                    )
                    term = jnp.dot(left, right, preferred_element_type=jnp.float32)
                    summed = term if summed is None else summed + term
                result[chunk, pl.ds(first, group)] = summed.astype(jnp.bfloat16).reshape(group, wide, rows)
                return inner

            lax.fori_loop(0, part // group, outputs, 0)
            for off in reversed(range(half)) if far == 0 else range(half, blocks):
                send_block(off, chunk, back_copy)
        returned[chunk, me] = result[chunk, me]
        return carry

    lax.fori_loop(0, chunks, convolve, 0)

    out_load.wait()
    for chunk in range(chunks):
        for far in range(2):
            base = jnp.where(lower == (far == 0), 0, part)

            finish(returned.at[chunk, pl.ds(0, part - 1 + far)], sems.at[2 + chunks + 2 * chunk + far])
            chosen = pl.ds(base, part)
            gated = returned[chunk, chosen].astype(jnp.float32) * open_gate[chunk, chosen]
            gated = gated.astype(jnp.bfloat16).reshape(part * wide, rows).T
            weight = out_w[chosen, chunk].reshape(part * wide, model)
            term = jnp.dot(gated, weight, preferred_element_type=jnp.float32)
            if chunk + far > 0:
                term = total[...] + term
            if chunk + far < chunks:
                total[...] = term
            else:
                mixed_ref[...] = term.astype(jnp.bfloat16)
    finish(lags.at[pl.ds(0, n - 1)], lag_sems.at[0])
    for sent in range(2):
        finish(returned.at[:, pl.ds(0, n - 1)], sems.at[sent])


def body(tokens, value_weight, gate_weight, out_weight, kernel_weight, kernel_bias):
    rows, model = tokens.shape
    heads = kernel_weight.shape[1]
    n = lax.axis_size("seq")
    width = model // n
    chunks = max(1, min(CHUNKS, width // 16))
    wide = width // chunks
    length = rows * n
    per = BLOCK // width
    half = jnp.bfloat16
    operands = (
        tokens,
        value_weight,
        gate_weight,
        out_weight.reshape(n, chunks, wide, model),
        kernel_weight.T,
        kernel_bias.reshape(1, heads),
    )
    return pl.pallas_call(
        functools.partial(layer_kernel, n),
        out_shape=pltpu.VMEM((rows, model), half),
        in_specs=[pl.BlockSpec(memory_space=pl.ANY)] * len(operands),
        out_specs=pl.BlockSpec(memory_space=pltpu.VMEM),
        scratch_shapes=[
            pltpu.VMEM((rows, model), half),
            pltpu.VMEM((n // per, model, BLOCK), half),
            pltpu.VMEM((model, model), half),
            pltpu.VMEM((n, chunks, wide, model), half),
            pltpu.VMEM((heads, model), half),
            pltpu.VMEM((1, heads), jnp.float32),
            pltpu.VMEM((chunks, n, wide, rows), half),
            pltpu.VMEM((chunks, 2 * n, wide, rows), half),
            pltpu.VMEM((heads, rows // LANES, LANES), half),
            pltpu.VMEM((n, rows // LANES, LANES), half),
            pltpu.VMEM((LANES, length + rows), half),
            pltpu.VMEM((chunks, n, wide, rows), jnp.float32),
            pltpu.VMEM((chunks, n, wide, rows), half),
            pltpu.VMEM((chunks, n, wide, rows), half),
            pltpu.VMEM((rows, model), jnp.float32),
            pltpu.SemaphoreType.DMA((8 + n // per,)),
            pltpu.SemaphoreType.REGULAR((per.bit_length() + 1,)),
            pltpu.SemaphoreType.DMA((2,)),
            pltpu.SemaphoreType.DMA((2 + 3 * chunks,)),
        ],
        compiler_params=pltpu.CompilerParams(
            collective_id=0, has_side_effects=True, vmem_limit_bytes=48 * 2**20
        ),
    )(*[pltpu.with_memory_space_constraint(operand, pltpu.HBM) for operand in operands])


def solution(mesh):
    placed = (P(("grp", "seq"), None), P(), P(), P(), P(), P())
    return jax.shard_map(
        body, mesh=mesh, in_specs=placed, out_specs=P(("grp", "seq"), None), check_vma=False
    )
```
